32 devices in a mesh: gx: 8 (over z, y), gy: 4 (over x, core).
Axes of the slice: x: 2, y: 2, z: 4, core: 2. Of those that a mesh axis runs over, the one named last changes fastest.
Arguments:
- output_one: bfloat16 [300, 12, 1024], P(None, 'gy', 'gx'), may hold values from -6 to 6
- output_two: bfloat16 [300, 12, 1024], P(None, 'gy', 'gx'), may hold values from -6 to 6
- cotan_one: bfloat16 [300, 12, 1024], P(None, 'gy', 'gx'), may hold values from -6 to 6
- cotan_two: bfloat16 [300, 12, 1024], P(None, 'gy', 'gx'), may hold values from -6 to 6
- wet_list: int32 [4, 8, 8, 48], P('gy', 'gx'), may hold values from -1 to 383, as said below
- depth_kernel: bfloat16 [300, 7, 7], replicated, may hold values from -0.875 to 0.875
- expand_weight: bfloat16 [300, 1200], replicated, may hold values from -0.375 to 0.375
- reduce_weight: bfloat16 [1200, 300], replicated, may hold values from -0.1875 to 0.1875
- level_expand: bfloat16 [4, 75, 300], replicated, may hold values from -0.75 to 0.75
- level_reduce: bfloat16 [4, 300, 75], replicated, may hold values from -0.375 to 0.375
Outputs:
- input_one: bfloat16 [300, 12, 1024], P(None, 'gy', 'gx')
- input_two: bfloat16 [300, 12, 1024], P(None, 'gy', 'gx')
- grad_input_one: bfloat16 [300, 12, 1024], P(None, 'gy', 'gx')
- grad_input_two: bfloat16 [300, 12, 1024], P(None, 'gy', 'gx')
- grad_kernel: float32 [300, 7, 7], replicated
- grad_expand: float32 [300, 1200], replicated
- grad_reduce: float32 [1200, 300], replicated
- grad_level_expand: float32 [4, 75, 300], replicated
- grad_level_reduce: float32 [4, 300, 75], replicated
The draws below stay inside these ranges and needn't reach their ends.
Inputs may be any that keep to these rules, and one draw needn't show every extreme that they name: wet_list[j, i, p, s] is -1 or a cell index row * 128 + column inside the tile at gy index j and gx index i, listed for owner p of the same latitude row of tiles; the indices listed by one tile are distinct and are exactly its wet cells; a tile lists at most 48 cells for one owner, and one owner is listed at most 216 cells by all tiles of its row together.
All inputs are finite; a program needn't handle non-finite values.
Results may differ from the reference program's by a relative error of at most 0.0078.
Values may be sent and summed in bfloat16 or wider, within the bound.
A program may use at most 128 MiB of HBM per device.

```python
import math
import jax
import jax.numpy as jnp
from jax import lax

VARS = 4
LEVELS = 75
CH = 300
HID = 1200
GEXP = 300
H_DEV = 3
W_DEV = 128
CELLS = 384
NY = 12
NX = 1024
SLOT = 48
N_GX = 8
N_GY = 4


def draw_wet_list(key, part):

    def one_row(row_key):
        row_keys = jax.random.split(row_key, 4)
        half_slot = SLOT // 2
        heavy_tile = jax.random.randint(row_keys[0], (), 0, N_GX)
        busy_owner = jax.random.randint(row_keys[1], (), 0, N_GX)
        counts = jax.random.randint(row_keys[2], (N_GX, N_GX), 0, half_slot + 1)
        source = jnp.arange(N_GX, dtype=jnp.int32)[:, None]
        target = jnp.arange(N_GX, dtype=jnp.int32)[None, :]
        counts = jnp.where(target == busy_owner, half_slot, counts)
        counts = jnp.where(source == heavy_tile, SLOT, counts)

        def one_tile(tile_key, tile_counts):
            shuffled = jax.random.permutation(tile_key, CELLS).astype(jnp.int32)
            offsets = jnp.cumsum(tile_counts) - tile_counts
            slot_ids = jnp.arange(SLOT, dtype=jnp.int32)
            position = jnp.clip(offsets[:, None] + slot_ids[None, :], 0, CELLS - 1)
            return jnp.where(slot_ids[None, :] < tile_counts[:, None], shuffled[position], -1).astype(jnp.int32)
        return jax.vmap(one_tile)(jax.random.split(row_keys[3], N_GX), counts)
    return jax.vmap(one_row)(jax.random.split(key, N_GY))


def steps_of(rng, extent, cuts, low, top_value):
    loudness = 1.0
    for dim, blocks in cuts:
        steps = jax.random.uniform(jax.random.fold_in(jax.random.fold_in(rng, 6), dim), (blocks,), jnp.float32, low / len(cuts), top_value / len(cuts))
        loudness = loudness * jnp.repeat(jnp.exp(steps), extent[dim] // blocks).reshape((-1,) + (1,) * (len(extent) - 1 - dim))
    return loudness


def gaussian(stream_key, extent, width, bound, pieces=(), kind=jnp.bfloat16):
    entries = jax.random.normal(stream_key, extent, jnp.float32) * width
    if len(pieces) > 0:
        entries = steps_of(stream_key, extent, pieces, -0.22, 0.18) * entries
    return jnp.clip(entries, min=-bound, max=bound).astype(kind)


def setup_inputs(seed: int = 0) -> dict:
    key_list = jax.random.split(jax.random.key(seed), 11)
    return {
        "output_one": gaussian(key_list[0], (CH, NY, NX), 1.0, 6.0, ((1, 4), (2, 8))),
        "output_two": gaussian(key_list[1], (CH, NY, NX), 1.0, 6.0, ((1, 4), (2, 8))),
        "cotan_one": gaussian(key_list[2], (CH, NY, NX), 1.0, 6.0, ((1, 4), (2, 8))),
        "cotan_two": gaussian(key_list[3], (CH, NY, NX), 1.0, 6.0, ((1, 4), (2, 8))),
        "wet_list": draw_wet_list(jax.random.fold_in(key_list[10], 71), 0),
        "depth_kernel": gaussian(key_list[5], (CH, 7, 7), 49 ** -0.5, 0.875),
        "expand_weight": gaussian(key_list[6], (CH, HID), CH ** -0.5, 0.375),
        "reduce_weight": gaussian(key_list[7], (HID, CH), HID ** -0.5, 0.1875),
        "level_expand": gaussian(key_list[8], (VARS, LEVELS, GEXP), LEVELS ** -0.5, 0.75),
        "level_reduce": gaussian(key_list[9], (VARS, GEXP, LEVELS), GEXP ** -0.5, 0.375),
    }


EPSILON = 1e-06

def gelu_slope(argument):
    normal_cdf = 0.5 * (1.0 + lax.erf(argument * 0.7071067811865476))
    return normal_cdf + argument * jnp.exp(-0.5 * argument * argument) * 0.3989422804014327

def wet_field(wet_list):
    tile_ny, tile_nx, owner_count, slot_count = wet_list.shape
    tile_cells = H_DEV * W_DEV
    listing = wet_list.reshape(tile_ny, tile_nx, owner_count * slot_count)
    target = jnp.where(listing >= 0, listing, tile_cells).astype(jnp.int32)
    row_ids = jnp.arange(tile_ny, dtype=jnp.int32)[:, None, None]
    col_ids = jnp.arange(tile_nx, dtype=jnp.int32)[None, :, None]
    tile_grid = jnp.zeros((tile_ny, tile_nx, tile_cells + 1), jnp.float32)
    tile_grid = tile_grid.at[row_ids, col_ids, target].set(1.0)
    tile_grid = tile_grid[:, :, :tile_cells].reshape(tile_ny, tile_nx, H_DEV, W_DEV)
    return tile_grid.transpose(0, 2, 1, 3).reshape(tile_ny * H_DEV, tile_nx * W_DEV)

def level_block(first_in, second, cot_first, cot_second, cell_mask, level_expand, level_reduce):
    groups, levels, expand_width = level_expand.shape
    block_size = first_in.shape[1]
    grouped = first_in.reshape(groups, levels, block_size).astype(jnp.float32)
    expand_wide = level_expand.astype(jnp.float32)
    reduce_wide = level_reduce.astype(jnp.float32)
    level_pre = jnp.einsum('gls,gle->ges', grouped, expand_wide)
    active = jax.nn.gelu(level_pre, approximate=False).astype(jnp.bfloat16)
    mixed_out = jnp.einsum('ges,gel->gls', active.astype(jnp.float32), reduce_wide)
    mixed_out = mixed_out.reshape(groups * levels, block_size) * cell_mask[None, :]
    rebuilt = (second.astype(jnp.float32) - mixed_out).astype(jnp.bfloat16)
    upstream = (cot_second * cell_mask.astype(jnp.bfloat16)[None, :]).reshape(groups, levels, block_size)
    back_act = jnp.einsum('gls,gel->ges', upstream.astype(jnp.float32), reduce_wide)
    back_pre = (back_act * gelu_slope(level_pre)).astype(jnp.bfloat16)
    back_in = jnp.einsum('ges,gle->gls', back_pre.astype(jnp.float32), expand_wide)
    total_one = (cot_first.astype(jnp.float32) + back_in.reshape(groups * levels, block_size)).astype(jnp.bfloat16)
    grad_in = jnp.einsum('gls,ges->gle', grouped, back_pre.astype(jnp.float32))
    grad_out = jnp.einsum('ges,gls->gel', active.astype(jnp.float32), upstream.astype(jnp.float32))
    return (rebuilt, total_one, grad_in, grad_out)

def mixer_block(spread, total_one, first_in, cell_mask, expand_weight, reduce_weight):
    center = spread - lax.optimization_barrier(jnp.mean(spread, axis=0, keepdims=True))
    rescale = lax.rsqrt(lax.optimization_barrier(jnp.mean(center * center, axis=0, keepdims=True)) + EPSILON)
    normal = center * rescale
    normal_half = normal.astype(jnp.bfloat16)
    hidden_pre = jnp.dot(expand_weight.T, normal_half, preferred_element_type=jnp.float32)
    hidden = jax.nn.gelu(hidden_pre, approximate=False).astype(jnp.bfloat16)
    update = jnp.dot(reduce_weight.T, hidden, preferred_element_type=jnp.float32)
    rebuilt_one = (first_in.astype(jnp.float32) - update * cell_mask[None, :]).astype(jnp.bfloat16)
    upstream = total_one * cell_mask.astype(jnp.bfloat16)[None, :]
    grad_reduce = jnp.dot(hidden, upstream.T, preferred_element_type=jnp.float32)
    back_hidden = jnp.dot(reduce_weight, upstream, preferred_element_type=jnp.float32)
    back_pre = (back_hidden * gelu_slope(hidden_pre)).astype(jnp.bfloat16)
    grad_expand = jnp.dot(normal_half, back_pre.T, preferred_element_type=jnp.float32)
    back_normal = jnp.dot(expand_weight, back_pre, preferred_element_type=jnp.float32)
    mean_back = lax.optimization_barrier(jnp.mean(back_normal, axis=0, keepdims=True))
    mean_cross = lax.optimization_barrier(jnp.mean(back_normal * normal, axis=0, keepdims=True))
    back_spread = (rescale * (back_normal - mean_back - normal * mean_cross)).astype(jnp.bfloat16)
    return (rebuilt_one, back_spread, grad_expand, grad_reduce)

def extend_field(field_in):
    grid_rows = field_in.shape[1]
    wrapped = jnp.concatenate([field_in[:, :, -3:], field_in, field_in[:, :, :3]], axis=2)
    south_rows = jnp.zeros_like(wrapped[:, :3, :])
    north_rows = wrapped[:, grid_rows - 3:, :][:, ::-1, ::-1]
    return jnp.concatenate([south_rows, wrapped, north_rows], axis=1)

def gather_back(grad_pad, grid_rows, grid_cols):
    inner = grad_pad[:, 3:grid_rows + 3, :]
    north_rows = grad_pad[:, grid_rows + 3:, :][:, ::-1, ::-1]
    inner = inner.at[:, grid_rows - 3:, :].add(north_rows)
    own_part = inner[:, :, 3:grid_cols + 3]
    own_part = own_part.at[:, :, grid_cols - 3:].add(inner[:, :, :3])
    own_part = own_part.at[:, :, :3].add(inner[:, :, grid_cols + 3:])
    return own_part

def reference(output_one, output_two, cotan_one, cotan_two, wet_list, depth_kernel, expand_weight, reduce_weight, level_expand, level_reduce):
    channels, grid_rows, grid_cols = output_one.shape
    grid_cells = grid_rows * grid_cols
    block_size = math.gcd(grid_cells, 4096)
    block_count = grid_cells // block_size
    wet_mask = wet_field(wet_list).reshape(grid_cells)

    def blocks(values_in):
        return values_in.reshape(values_in.shape[0], block_count, block_size).transpose(1, 0, 2)

    def unblock(values_in):
        return values_in.transpose(1, 0, 2).reshape(values_in.shape[1], block_count * block_size)
    flat_one = output_one.reshape(channels, grid_cells)
    flat_two = output_two.reshape(channels, grid_cells)
    flat_cot_one = cotan_one.reshape(channels, grid_cells)
    flat_cot_two = cotan_two.reshape(channels, grid_cells)
    mask_blocks = wet_mask.reshape(block_count, block_size)

    def level_step(running, inputs_now):
        first_in, second, cot_first, cot_second, cell_mask = inputs_now
        rebuilt, total_one, grad_in, grad_out = level_block(first_in, second, cot_first, cot_second, cell_mask, level_expand, level_reduce)
        return ((running[0] + grad_in, running[1] + grad_out), (rebuilt, total_one))
    level_zero = (jnp.zeros(level_expand.shape, jnp.float32), jnp.zeros(level_reduce.shape, jnp.float32))
    level_sums, level_outs = lax.scan(level_step, level_zero, (blocks(flat_one), blocks(flat_two), blocks(flat_cot_one), blocks(flat_cot_two), mask_blocks))
    input_two = unblock(level_outs[0]).reshape(channels, grid_rows, grid_cols)
    total_flat = unblock(level_outs[1])
    padded = extend_field(input_two)
    wide_field = padded.astype(jnp.float32)
    kernel_wide = depth_kernel.astype(jnp.float32)
    spread = jnp.zeros((channels, grid_rows, grid_cols), jnp.float32)
    for row_tap in range(7):
        for col_tap in range(7):
            spread = spread + kernel_wide[:, row_tap, col_tap][:, None, None] * wide_field[:, row_tap:row_tap + grid_rows, col_tap:col_tap + grid_cols]

    def mixer_step(running, inputs_now):
        spread_now, total_now, first_in, cell_mask = inputs_now
        rebuilt_one, back_spread, grad_expand, grad_reduce = mixer_block(spread_now, total_now, first_in, cell_mask, expand_weight, reduce_weight)
        return ((running[0] + grad_expand, running[1] + grad_reduce), (rebuilt_one, back_spread))
    mixer_zero = (jnp.zeros(expand_weight.shape, jnp.float32), jnp.zeros(reduce_weight.shape, jnp.float32))
    mixer_sums, mixer_outs = lax.scan(mixer_step, mixer_zero, (blocks(spread.reshape(channels, grid_cells)), blocks(total_flat), blocks(flat_one), mask_blocks))
    input_one = unblock(mixer_outs[0]).reshape(channels, grid_rows, grid_cols)
    back_field = unblock(mixer_outs[1]).reshape(channels, grid_rows, grid_cols).astype(jnp.float32)
    tap_rows = []
    for row_tap in range(7):
        tap_cols = []
        for col_tap in range(7):
            tap_cols.append(lax.optimization_barrier(jnp.sum(back_field * wide_field[:, row_tap:row_tap + grid_rows, col_tap:col_tap + grid_cols], axis=(1, 2))))
        tap_rows.append(jnp.stack(tap_cols, axis=1))
    grad_kernel = jnp.stack(tap_rows, axis=1)
    grad_pad = jnp.zeros((channels, grid_rows + 6, grid_cols + 6), jnp.float32)
    for row_tap in range(7):
        for col_tap in range(7):
            term = kernel_wide[:, row_tap, col_tap][:, None, None] * back_field
            grad_pad = grad_pad + jnp.pad(term, ((0, 0), (row_tap, 6 - row_tap), (col_tap, 6 - col_tap)))
    through = gather_back(grad_pad, grid_rows, grid_cols)
    grad_input_two = (cotan_two.astype(jnp.float32) + through).astype(jnp.bfloat16)
    grad_input_one = total_flat.reshape(channels, grid_rows, grid_cols)
    factor = 1.0 / math.sqrt(grid_cells)
    return (input_one, input_two, grad_input_one, grad_input_two, grad_kernel * factor, mixer_sums[0] * factor, mixer_sums[1] * factor, level_sums[0] * factor, level_sums[1] * factor)
```

```python
import functools
import math

import jax
import jax.numpy as jnp
import numpy as np
from jax import lax
from jax.experimental import pallas as pl
from jax.experimental.pallas import tpu as pltpu
from jax.sharding import PartitionSpec as P

EPSILON = 1e-06
MESH = pl.DeviceIdType.MESH
F32 = jnp.float32
BF16 = jnp.bfloat16
REACH = 3
TAPS = 7
EDGE_ROWS = 16
WEST, EAST, NORTH_WEST, NORTH_EAST, SOUTH_WEST, SOUTH_EAST = range(6)


def dot(a, b, ca, cb):
    return lax.dot_general(a, b, (((ca,), (cb,)), ((), ())), preferred_element_type=F32)


def activate(pre_ref, back_ref, act_ref, bp_ref):
    def step(i, carry):
        rows = pl.ds(pl.multiple_of(i * 16, 16), 16)
        t = pre_ref[rows, :]
        cdf = 0.5 * (1.0 + lax.erf(t * 0.7071067811865476))
        act_ref[rows, :] = (t * cdf).astype(BF16)
        slope = cdf + t * jnp.exp(-0.5 * t * t) * 0.3989422804014327
        bp_ref[rows, :] = (back_ref[rows, :] * slope).astype(BF16)
        return carry

    lax.fori_loop(0, pre_ref.shape[0] // 16, step, 0)


def level_kernel(
    factor, slot, one, two, cot_one, cot_two, listing, le, lr, pick_left, pick_right,
    two_out, total_out, left_out, right_out, mask_out, gle, glr,
    a, b, c, d, pre, back, act, bp,
):
    groups, levels, width = le.shape
    channels, cells = one.shape
    entries = listing[...]
    cell_ids = lax.broadcasted_iota(jnp.int32, (entries.shape[0], cells), 1)
    hit = jnp.where(entries == cell_ids, 1.0, 0.0)
    mask = jnp.max(hit, axis=0, keepdims=True)
    mask_out[...] = jnp.broadcast_to(mask, mask_out.shape)
    a[...] = one[...].astype(F32)
    b[...] = cot_two[...].astype(F32) * mask
    for v in range(groups):
        g = a[v * levels : (v + 1) * levels, :].astype(BF16)
        u = b[v * levels : (v + 1) * levels, :].astype(BF16)
        pre[v * slot : v * slot + width, :] = dot(le[v], g, 0, 0)
        back[v * slot : v * slot + width, :] = dot(lr[v], u, 1, 0)
    activate(pre, back, act, bp)
    for v in range(groups):
        g = a[v * levels : (v + 1) * levels, :].astype(BF16)
        u = b[v * levels : (v + 1) * levels, :].astype(BF16)
        act_v = act[v * slot : v * slot + width, :]
        bp_v = bp[v * slot : v * slot + width, :]
        c[v * levels : (v + 1) * levels, :] = dot(lr[v], act_v, 0, 0)
        d[v * levels : (v + 1) * levels, :] = dot(le[v], bp_v, 1, 0)
        gle[v] = (dot(g, bp_v, 1, 1) * factor).astype(BF16)
        glr[v] = (dot(act_v, u, 1, 1) * factor).astype(BF16)
    rebuilt = (two[...].astype(F32) - c[...] * mask).astype(BF16)
    two_out[...] = rebuilt
    total_out[...] = (cot_one[...].astype(F32) + d[...]).astype(BF16)
    left_out[...] = dot(pick_left[...], rebuilt, 1, 1).astype(BF16)
    right_out[...] = dot(pick_right[...], rebuilt, 1, 1).astype(BF16)


def halo_kernel(nx, ny, tile, left, right, north, south, edges, send_sem, recv_sem):
    i = lax.axis_index("gx")
    j = lax.axis_index("gy")
    east, west = lax.rem(i + 1, nx), lax.rem(i + nx - 1, nx)
    mirror = nx - 1 - i
    beyond, before = lax.rem(mirror + 1, nx), lax.rem(mirror + nx - 1, nx)
    top = j == ny - 1
    inner = j < ny - 1
    raised = j > 0

    sends = [
        (None, right, edges.at[WEST], 0, east, j),
        (None, left, edges.at[EAST], 1, west, j),
        (raised, tile, north, 2, i, j - 1),
        (raised, right, edges.at[NORTH_WEST], 3, east, j - 1),
        (raised, left, edges.at[NORTH_EAST], 4, west, j - 1),
        (inner, tile, south, 5, i, j + 1),
        (inner, right, edges.at[SOUTH_WEST], 6, east, j + 1),
        (inner, left, edges.at[SOUTH_EAST], 7, west, j + 1),
        (top, tile, north, 2, mirror, j),
        (top & (beyond != i), left, edges.at[NORTH_WEST], 3, beyond, j),
        (top & (before != i), right, edges.at[NORTH_EAST], 4, before, j),
    ]

    def guarded(active, run):
        if active is None:
            run()
        else:
            pl.when(active)(run)

    def copy_of(k):
        active, source, target, number, x, y = sends[k]
        return pltpu.make_async_remote_copy(
            src_ref=source,
            dst_ref=target,
            send_sem=send_sem.at[k],
            recv_sem=recv_sem.at[number],
            device_id=(x, y),
            device_id_type=MESH,
        )

    barrier = pltpu.get_barrier_semaphore()
    for active, _, _, _, x, y in sends:

        def tell(x=x, y=y):
            pl.semaphore_signal(barrier, inc=1, device_id=(x, y), device_id_type=MESH)

        guarded(active, tell)
    one_if = lambda flag: flag.astype(jnp.int32)
    peers = 5 + 3 * one_if(raised) - one_if(top & (beyond == i)) - one_if(top & (before == i))
    pl.semaphore_wait(barrier, peers)
    order = [2, 5, 8, 0, 1, 3, 4, 6, 7, 9, 10]
    for k in order:
        guarded(sends[k][0], lambda k=k: copy_of(k).start())

    @pl.when(top & (beyond == i))
    def _():
        edges[NORTH_WEST] = left[...]

    @pl.when(top & (before == i))
    def _():
        edges[NORTH_EAST] = right[...]

    for k in order:
        guarded(sends[k][0], lambda k=k: copy_of(k).wait_send())
    arrivals = [
        (None, 0), (None, 1), (raised, 5), (raised, 6), (raised, 7),
        (inner, 2), (inner, 3), (inner, 4), (top, 8),
        (top & (beyond != i), 9), (top & (before != i), 10),
    ]
    for active, k in arrivals:
        guarded(active, lambda k=k: copy_of(k).wait_recv())


def load_field(own, north, south, edges, turn, place_mid, place_north, place_south, flags, mid, rim):
    channels, cells = own.shape
    has_south = flags[0] > 0
    mid[0, :channels, :] = jnp.where(has_south, south[...].astype(F32), 0.0)
    mid[1, :channels, :] = own[...].astype(F32)
    mid[2, :channels, :] = dot(north[...], turn[...], 1, 0)
    pairs = (
        (SOUTH_WEST, SOUTH_EAST, place_south),
        (WEST, EAST, place_mid),
        (NORTH_WEST, NORTH_EAST, place_north),
    )
    for group, (west, east, place) in enumerate(pairs):
        side = dot(edges[west], place[0], 0, 0) + dot(edges[east], place[1], 0, 0)
        if group == 0:
            side = jnp.where(has_south, side, 0.0)
        rim[group, :channels, :] = side


def shifted_rows(mid, rim, rows, columns, offset):
    lane = lax.broadcasted_iota(jnp.int32, (8, columns), 1)
    out = []
    for p in range(9):
        cols = pl.ds((p % 3) * columns, columns)
        center = mid[p // 3, rows, cols]
        if offset == 0:
            out.append(center)
            continue
        side = rim[p // 3, rows, cols]
        outside = lane < offset if offset > 0 else lane >= columns + offset
        out.append(pltpu.roll(jnp.where(outside, side, center), (-offset) % columns, 1))
    return out


def convolve(mid, rim, weights, north_weights, out, columns):
    blocks = mid.shape[1] // 8

    def step(i, carry):
        rows = pl.ds(pl.multiple_of(i * 8, 8), 8)
        w = weights[rows, :]
        wn = north_weights[rows, :]
        acc = [jnp.zeros((8, columns), F32) for _ in range(3)]
        for col in range(TAPS):
            field = shifted_rows(mid, rim, rows, columns, col - REACH)
            for row in range(TAPS):
                t = row * TAPS + col
                k = jnp.broadcast_to(w[:, t : t + 1], (8, columns))
                kn = jnp.broadcast_to(wn[:, t : t + 1], (8, columns)) if row > 3 else None
                for r in range(3):
                    acc[r] = acc[r] + (kn if r + row >= 6 else k) * field[r + row]
        for r in range(3):
            out[rows, r * columns : (r + 1) * columns] = acc[r]
        return carry

    lax.fori_loop(0, blocks, step, 0)


def correlate(mid, rim, back, out, columns):
    blocks = mid.shape[1] // 8

    def step(i, carry):
        rows = pl.ds(pl.multiple_of(i * 8, 8), 8)
        lane = lax.broadcasted_iota(jnp.int32, (8, columns), 1)
        g = [back[rows, r * columns : (r + 1) * columns] for r in range(3)]
        total = jnp.zeros((8, columns), F32)
        for col in range(TAPS):
            field = shifted_rows(mid, rim, rows, columns, col - REACH)
            for row in range(TAPS):
                part = g[0] * field[row] + g[1] * field[row + 1] + g[2] * field[row + 2]
                summed = jnp.sum(part, axis=1, keepdims=True)
                total = jnp.where(lane == row * TAPS + col, summed, total)
        out[rows, :] = total
        return carry

    lax.fori_loop(0, blocks, step, 0)


def mixer_kernel(
    factor, columns, flags, own, north, south, edges, turn, place_mid, place_north, place_south,
    one, total, mask_in, weights, ew, rw, pick_left, pick_right,
    one_out, back_out, left_out, right_out, gk, ge, gr,
    mid, rim, spread, pre, back, act, bp, gk_wide,
):
    channels, cells = own.shape
    load_field(own, north, south, edges, turn, place_mid, place_north, place_south, flags, mid, rim)
    mask = mask_in[0:1, :]
    upstream = (total[...].astype(F32) * mask).astype(BF16)
    back[...] = dot(rw[...], upstream, 1, 0)
    convolve(mid, rim, weights, weights, spread, columns)
    field = spread[:channels, :]
    center = field - jnp.mean(field, axis=0, keepdims=True)
    rescale = lax.rsqrt(jnp.mean(center * center, axis=0, keepdims=True) + EPSILON)
    normal = center * rescale
    spread[:channels, :] = normal
    half = normal.astype(BF16)
    pre[...] = dot(ew[...], half, 0, 0)
    activate(pre, back, act, bp)
    back_normal = dot(ew[...], bp[...], 1, 0)
    normal = spread[:channels, :]
    mean_back = jnp.mean(back_normal, axis=0, keepdims=True)
    mean_cross = jnp.mean(back_normal * normal, axis=0, keepdims=True)
    back_spread = (rescale * (back_normal - mean_back - normal * mean_cross)).astype(BF16)
    back_out[...] = back_spread
    left_out[...] = dot(pick_left[...], back_spread, 1, 1).astype(BF16)
    right_out[...] = dot(pick_right[...], back_spread, 1, 1).astype(BF16)
    ge[...] = (dot(normal.astype(BF16), bp[...], 1, 1) * factor).astype(BF16)
    gr[...] = (dot(act[...], upstream, 1, 1) * factor).astype(BF16)
    update = dot(rw[...], act[...], 0, 0)
    one_out[...] = (one[...].astype(F32) - update * mask).astype(BF16)
    spread[:channels, :] = back_spread.astype(F32)
    correlate(mid, rim, spread, gk_wide, columns)
    gk[...] = (gk_wide[:channels, :] * factor).astype(BF16)


def back_kernel(
    columns, flags, own, north, south, edges, turn, place_mid, place_north, place_south,
    cot_two, weights, north_weights, out, mid, rim, through,
):
    channels, cells = own.shape
    load_field(own, north, south, edges, turn, place_mid, place_north, place_south, flags, mid, rim)
    convolve(mid, rim, weights, north_weights, through, columns)
    out[...] = (cot_two[...].astype(F32) + through[:channels, :]).astype(BF16)


def placements(rows, columns):
    cells = rows * columns
    pick_left = np.zeros((EDGE_ROWS, cells), np.float32)
    pick_right = np.zeros((EDGE_ROWS, cells), np.float32)
    place = np.zeros((2, EDGE_ROWS, cells), np.float32)
    folded = np.zeros((2, EDGE_ROWS, cells), np.float32)
    for r in range(rows):
        for c in range(REACH):
            e = r * REACH + c
            pick_left[e, r * columns + c] = 1
            pick_right[e, r * columns + columns - REACH + c] = 1
            place[0, e, r * columns + columns - REACH + c] = 1
            place[1, e, r * columns + c] = 1
            turned = rows - 1 - r
            folded[0, e, turned * columns + columns - 1 - c] = 1
            folded[1, e, turned * columns + REACH - 1 - c] = 1
    return pick_left, pick_right, place, folded


def body(
    output_one, output_two, cotan_one, cotan_two, wet_list, depth_kernel,
    expand_weight, reduce_weight, level_expand, level_reduce,
):
    channels, rows, columns = output_one.shape
    cells = rows * columns
    groups, levels, width = level_expand.shape
    hidden = expand_weight.shape[1]
    nx, ny = lax.axis_size("gx"), lax.axis_size("gy")
    factor = 1.0 / math.sqrt(cells * nx * ny)
    wide = -(-channels // 8) * 8
    slot = -(-width // 16) * 16
    i, j = lax.axis_index("gx"), lax.axis_index("gy")
    top = j == ny - 1
    flags = jnp.stack([(j > 0).astype(jnp.int32), top.astype(jnp.int32)])

    pick_left, pick_right, place, folded = [jnp.asarray(m, BF16) for m in placements(rows, columns)]
    place_north = jnp.where(top, folded, place)
    row_id = lax.broadcasted_iota(jnp.int32, (cells, cells), 0)
    col_id = lax.broadcasted_iota(jnp.int32, (cells, cells), 1)
    turn = jnp.where(jnp.where(top, cells - 1 - row_id, row_id) == col_id, 1.0, 0.0).astype(BF16)

    flat = lambda x: x.reshape(channels, cells)
    tile = jax.ShapeDtypeStruct((channels, cells), BF16)
    edge = jax.ShapeDtypeStruct((EDGE_ROWS, channels), BF16)
    vmem = pl.BlockSpec(memory_space=pltpu.VMEM)
    smem = pl.BlockSpec(memory_space=pltpu.SMEM)
    params = pltpu.CompilerParams(vmem_limit_bytes=56 * 1024 * 1024)

    one, two, cot_one, cot_two = flat(output_one), flat(output_two), flat(cotan_one), flat(cotan_two)
    two_in, total, left, right, mask, gle, glr = pl.pallas_call(
        functools.partial(level_kernel, factor, slot),
        out_shape=(
            tile, tile, edge, edge,
            jax.ShapeDtypeStruct((8, cells), F32),
            jax.ShapeDtypeStruct(level_expand.shape, BF16),
            jax.ShapeDtypeStruct(level_reduce.shape, BF16),
        ),
        in_specs=[vmem] * 9,
        out_specs=(vmem,) * 7,
        scratch_shapes=[pltpu.VMEM((channels, cells), F32)] * 4
        + [pltpu.VMEM((groups * slot, cells), F32)] * 2
        + [pltpu.VMEM((groups * slot, cells), BF16)] * 2,
        compiler_params=params,
        name="level",
    )(one, two, cot_one, cot_two, wet_list.reshape(-1, 1), level_expand, level_reduce, pick_left, pick_right)
    gle, glr = lax.psum((gle, glr), ("gx", "gy"))

    halo = pl.pallas_call(
        functools.partial(halo_kernel, nx, ny),
        out_shape=(tile, tile, jax.ShapeDtypeStruct((6, EDGE_ROWS, channels), BF16)),
        in_specs=[vmem] * 3,
        out_specs=(vmem,) * 3,
        scratch_shapes=[pltpu.SemaphoreType.DMA((11,)), pltpu.SemaphoreType.DMA((8,))],
        compiler_params=pltpu.CompilerParams(collective_id=0, has_side_effects=True),
        name="halo",
    )
    north, south, edges = halo(two_in, left, right)

    taps = depth_kernel.astype(F32).reshape(channels, TAPS * TAPS)
    pad = lambda w: jnp.pad(w, ((0, wide - channels), (0, 128 - TAPS * TAPS)))
    field_scratch = [pltpu.VMEM((3, wide, cells), F32)] * 2 + [pltpu.VMEM((wide, cells), F32)]
    one_in, back, back_left, back_right, gk, ge, gr = pl.pallas_call(
        functools.partial(mixer_kernel, factor, columns),
        out_shape=(
            tile, tile, edge, edge,
            jax.ShapeDtypeStruct((channels, 128), BF16),
            jax.ShapeDtypeStruct(expand_weight.shape, BF16),
            jax.ShapeDtypeStruct(reduce_weight.shape, BF16),
        ),
        in_specs=[smem] + [vmem] * 16,
        out_specs=(vmem,) * 7,
        scratch_shapes=field_scratch
        + [pltpu.VMEM((hidden, cells), F32)] * 2
        + [pltpu.VMEM((hidden, cells), BF16)] * 2
        + [pltpu.VMEM((wide, 128), F32)],
        compiler_params=params,
        name="mixer",
    )(
        flags, two_in, north, south, edges, turn, place, place_north, place, one, total, mask,
        pad(taps), expand_weight, reduce_weight, pick_left, pick_right,
    )
    gk, ge, gr = lax.psum((gk, ge, gr), ("gx", "gy"))

    north, south, edges = halo(back, back_left, back_right)
    flipped = taps[:, ::-1]
    grad_two = pl.pallas_call(
        functools.partial(back_kernel, columns),
        out_shape=tile,
        in_specs=[smem] + [vmem] * 11,
        out_specs=vmem,
        scratch_shapes=field_scratch,
        compiler_params=params,
        name="back",
    )(
        flags, back, north, south, edges, turn, place, place_north, place, cot_two,
        pad(flipped), pad(jnp.where(top, taps, flipped)),
    )
    grid = lambda x: x.reshape(channels, rows, columns)
    gk = gk[:, : TAPS * TAPS].astype(F32).reshape(channels, TAPS, TAPS)
    return (
        grid(one_in), grid(two_in), grid(total), grid(grad_two),
        gk, ge.astype(F32), gr.astype(F32), gle.astype(F32), glr.astype(F32),
    )


def solution(mesh):
    field = P(None, "gy", "gx")
    return jax.shard_map(
        body,
        mesh=mesh,
        in_specs=(field,) * 4 + (P("gy", "gx", None, None),) + (P(),) * 5,
        out_specs=(field,) * 4 + (P(),) * 5,
        check_vma=False,
    )
```

```python
import functools
import math

import jax
import jax.numpy as jnp
import numpy as np
from jax import lax
from jax.experimental import pallas as pl
from jax.experimental.pallas import tpu as pltpu
from jax.sharding import PartitionSpec as P

EPSILON = 1e-06
MESH = pl.DeviceIdType.MESH
F32 = jnp.float32
BF16 = jnp.bfloat16
REACH = 3
TAPS = 7
EDGE_ROWS = 16
WEST, EAST, NORTH_WEST, NORTH_EAST, SOUTH_WEST, SOUTH_EAST = range(6)


def dot(a, b, ca, cb):
    return lax.dot_general(a, b, (((ca,), (cb,)), ((), ())), preferred_element_type=F32)


def activate(pre_ref, back_ref, act_ref, bp_ref):
    def step(i, carry):
        rows = pl.ds(pl.multiple_of(i * 16, 16), 16)
        t = pre_ref[rows, :]
        cdf = 0.5 * (1.0 + lax.erf(t * 0.7071067811865476))
        act_ref[rows, :] = (t * cdf).astype(BF16)
        slope = cdf + t * jnp.exp(-0.5 * t * t) * 0.3989422804014327
        bp_ref[rows, :] = (back_ref[rows, :] * slope).astype(BF16)
        return carry

    lax.fori_loop(0, pre_ref.shape[0] // 16, step, 0)


def level_kernel(
    factor, slot, one, two, cot_one, cot_two, listing, le, lr, pick_left, pick_right,
    two_out, total_out, left_out, right_out, mask_out, gle, glr,
    a, b, c, d, pre, back, act, bp,
):
    groups, levels, width = le.shape
    channels, cells = one.shape
    entries = listing[...]
    cell_ids = lax.broadcasted_iota(jnp.int32, (entries.shape[0], cells), 1)
    hit = jnp.where(entries == cell_ids, 1.0, 0.0)
    mask = jnp.max(hit, axis=0, keepdims=True)
    mask_out[...] = jnp.broadcast_to(mask, mask_out.shape)
    a[...] = one[...].astype(F32)
    b[...] = cot_two[...].astype(F32) * mask
    for v in range(groups):
        g = a[v * levels : (v + 1) * levels, :].astype(BF16)
        u = b[v * levels : (v + 1) * levels, :].astype(BF16)
        pre[v * slot : v * slot + width, :] = dot(le[v], g, 0, 0)
        back[v * slot : v * slot + width, :] = dot(lr[v], u, 1, 0)
    activate(pre, back, act, bp)
    for v in range(groups):
        g = a[v * levels : (v + 1) * levels, :].astype(BF16)
        u = b[v * levels : (v + 1) * levels, :].astype(BF16)
        act_v = act[v * slot : v * slot + width, :]
        bp_v = bp[v * slot : v * slot + width, :]
        c[v * levels : (v + 1) * levels, :] = dot(lr[v], act_v, 0, 0)
        d[v * levels : (v + 1) * levels, :] = dot(le[v], bp_v, 1, 0)
        gle[v] = dot(g, bp_v, 1, 1) * factor
        glr[v] = dot(act_v, u, 1, 1) * factor
    rebuilt = (two[...].astype(F32) - c[...] * mask).astype(BF16)
    two_out[...] = rebuilt
    total_out[...] = (cot_one[...].astype(F32) + d[...]).astype(BF16)
    left_out[...] = dot(pick_left[...], rebuilt, 1, 1).astype(BF16)
    right_out[...] = dot(pick_right[...], rebuilt, 1, 1).astype(BF16)


def halo_kernel(nx, ny, tile, left, right, north, south, edges, send_sem, recv_sem):
    i = lax.axis_index("gx")
    j = lax.axis_index("gy")
    east, west = lax.rem(i + 1, nx), lax.rem(i + nx - 1, nx)
    mirror = nx - 1 - i
    beyond, before = lax.rem(mirror + 1, nx), lax.rem(mirror + nx - 1, nx)
    top = j == ny - 1
    inner = j < ny - 1
    raised = j > 0

    sends = [
        (None, right, edges.at[WEST], 0, east, j),
        (None, left, edges.at[EAST], 1, west, j),
        (raised, tile, north, 2, i, j - 1),
        (raised, right, edges.at[NORTH_WEST], 3, east, j - 1),
        (raised, left, edges.at[NORTH_EAST], 4, west, j - 1),
        (inner, tile, south, 5, i, j + 1),
        (inner, right, edges.at[SOUTH_WEST], 6, east, j + 1),
        (inner, left, edges.at[SOUTH_EAST], 7, west, j + 1),
        (top, tile, north, 2, mirror, j),
        (top & (beyond != i), left, edges.at[NORTH_WEST], 3, beyond, j),
        (top & (before != i), right, edges.at[NORTH_EAST], 4, before, j),
    ]

    def guarded(active, run):
        if active is None:
            run()
        else:
            pl.when(active)(run)

    def copy_of(k):
        active, source, target, number, x, y = sends[k]
        return pltpu.make_async_remote_copy(
            src_ref=source,
            dst_ref=target,
            send_sem=send_sem.at[k],
            recv_sem=recv_sem.at[number],
            device_id=(x, y),
            device_id_type=MESH,
        )

    barrier = pltpu.get_barrier_semaphore()
    for active, _, _, _, x, y in sends:

        def tell(x=x, y=y):
            pl.semaphore_signal(barrier, inc=1, device_id=(x, y), device_id_type=MESH)

        guarded(active, tell)
    one_if = lambda flag: flag.astype(jnp.int32)
    peers = 5 + 3 * one_if(raised) - one_if(top & (beyond == i)) - one_if(top & (before == i))
    pl.semaphore_wait(barrier, peers)
    order = [2, 5, 8, 0, 1, 3, 4, 6, 7, 9, 10]
    for k in order:
        guarded(sends[k][0], lambda k=k: copy_of(k).start())

    @pl.when(top & (beyond == i))
    def _():
        edges[NORTH_WEST] = left[...]

    @pl.when(top & (before == i))
    def _():
        edges[NORTH_EAST] = right[...]

    for k in order:
        guarded(sends[k][0], lambda k=k: copy_of(k).wait_send())
    arrivals = [
        (None, 0), (None, 1), (raised, 5), (raised, 6), (raised, 7),
        (inner, 2), (inner, 3), (inner, 4), (top, 8),
        (top & (beyond != i), 9), (top & (before != i), 10),
    ]
    for active, k in arrivals:
        guarded(active, lambda k=k: copy_of(k).wait_recv())


def sum_kernel(dims, pack, out, work, held, send_sem, recv_sem):
    place = (lax.axis_index("gx"), lax.axis_index("gy"))
    steps = len(dims)
    lanes = pack.shape[2] // 3
    bits, peers = [], []
    for axis, k in dims:
        bit = lax.rem(place[axis] // (1 << k), 2)
        bits.append(bit)
        other = place[axis] + (1 - 2 * bit) * (1 << k)
        peers.append((other, place[1]) if axis == 0 else (place[0], other))
    barrier = pltpu.get_barrier_semaphore()
    for peer in peers:
        pl.semaphore_signal(barrier, inc=1, device_id=peer, device_id_type=MESH)
    pl.semaphore_wait(barrier, steps)
    rest = steps - 1
    orders = [[0] + [1 + (k + s) % rest for k in range(rest)] for s in range(3)]
    base = [0, 0, 0]
    trail = []
    size = pack.shape[0]
    offset = 0
    for step in range(steps):
        size //= 2
        copies = []
        source = pack if step == 0 else work
        target = out if step == steps - 1 else work
        ranges = []
        for s in range(3):
            d = orders[s][step]
            cols = pl.ds(s * lanes, lanes)
            keep = base[s] + bits[d] * size
            give = base[s] + (1 - bits[d]) * size
            ranges.append((keep, give))
            copy = pltpu.make_async_remote_copy(
                src_ref=source.at[pl.ds(give, size), :, cols],
                dst_ref=held.at[pl.ds(offset, size), :, cols],
                send_sem=send_sem.at[s, step],
                recv_sem=recv_sem.at[s, step],
                device_id=peers[d],
                device_id_type=MESH,
            )
            copy.start()
            copies.append(copy)
        for s in range(3):
            copies[s].wait_recv()
            cols = pl.ds(s * lanes, lanes)
            keep = ranges[s][0]

            def add(c, carry, cols=cols, keep=keep, source=source, target=target, offset=offset):
                mine = source[keep + c, :, cols].astype(F32)
                target[keep + c, :, cols] = (mine + held[offset + c, :, cols].astype(F32)).astype(BF16)
                return carry

            lax.fori_loop(0, size, add, 0)
            base[s] = keep
        for copy in copies:
            copy.wait_send()
        trail.append((size, ranges))
        offset += size
    for step in reversed(range(steps)):
        size, ranges = trail[step]
        copies = []
        for s in range(3):
            cols = pl.ds(s * lanes, lanes)
            part = out.at[pl.ds(ranges[s][0], size), :, cols]
            copy = pltpu.make_async_remote_copy(
                src_ref=part,
                dst_ref=part,
                send_sem=send_sem.at[s, steps + step],
                recv_sem=recv_sem.at[s, steps + step],
                device_id=peers[orders[s][step]],
                device_id_type=MESH,
            )
            copy.start()
            copies.append(copy)
        for copy in copies:
            copy.wait()


def load_field(own, north, south, edges, turn, place_mid, place_north, place_south, flags, mid, rim):
    channels, cells = own.shape
    has_south = flags[0] > 0
    mid[0, :channels, :] = jnp.where(has_south, south[...].astype(F32), 0.0)
    mid[1, :channels, :] = own[...].astype(F32)
    mid[2, :channels, :] = dot(north[...], turn[...], 1, 0)
    pairs = (
        (SOUTH_WEST, SOUTH_EAST, place_south),
        (WEST, EAST, place_mid),
        (NORTH_WEST, NORTH_EAST, place_north),
    )
    for group, (west, east, place) in enumerate(pairs):
        side = dot(edges[west], place[0], 0, 0) + dot(edges[east], place[1], 0, 0)
        if group == 0:
            side = jnp.where(has_south, side, 0.0)
        rim[group, :channels, :] = side


def shifted_rows(mid, rim, rows, columns, offset):
    lane = lax.broadcasted_iota(jnp.int32, (8, columns), 1)
    out = []
    for p in range(9):
        cols = pl.ds((p % 3) * columns, columns)
        center = mid[p // 3, rows, cols]
        if offset == 0:
            out.append(center)
            continue
        side = rim[p // 3, rows, cols]
        outside = lane < offset if offset > 0 else lane >= columns + offset
        out.append(pltpu.roll(jnp.where(outside, side, center), (-offset) % columns, 1))
    return out


def convolve(mid, rim, weights, north_weights, out, columns):
    blocks = mid.shape[1] // 8

    def step(i, carry):
        rows = pl.ds(pl.multiple_of(i * 8, 8), 8)
        w = weights[rows, :]
        wn = north_weights[rows, :]
        acc = [jnp.zeros((8, columns), F32) for _ in range(3)]
        for col in range(TAPS):
            field = shifted_rows(mid, rim, rows, columns, col - REACH)
            for row in range(TAPS):
                t = row * TAPS + col
                k = jnp.broadcast_to(w[:, t : t + 1], (8, columns))
                kn = jnp.broadcast_to(wn[:, t : t + 1], (8, columns)) if row > 3 else None
                for r in range(3):
                    acc[r] = acc[r] + (kn if r + row >= 6 else k) * field[r + row]
        for r in range(3):
            out[rows, r * columns : (r + 1) * columns] = acc[r]
        return carry

    lax.fori_loop(0, blocks, step, 0)


def correlate(mid, rim, back, out, columns):
    blocks = mid.shape[1] // 8

    def step(i, carry):
        rows = pl.ds(pl.multiple_of(i * 8, 8), 8)
        lane = lax.broadcasted_iota(jnp.int32, (8, columns), 1)
        g = [back[rows, r * columns : (r + 1) * columns] for r in range(3)]
        total = jnp.zeros((8, columns), F32)
        for col in range(TAPS):
            field = shifted_rows(mid, rim, rows, columns, col - REACH)
            for row in range(TAPS):
                part = g[0] * field[row] + g[1] * field[row + 1] + g[2] * field[row + 2]
                summed = jnp.sum(part, axis=1, keepdims=True)
                total = jnp.where(lane == row * TAPS + col, summed, total)
        out[rows, :] = total
        return carry

    lax.fori_loop(0, blocks, step, 0)


def mixer_kernel(
    factor, columns, flags, own, north, south, edges, turn, place_mid, place_north, place_south,
    one, total, mask_in, weights, ew, rw, pick_left, pick_right,
    one_out, back_out, left_out, right_out, pack,
    mid, rim, spread, pre, back, act, bp, gk_wide,
):
    channels, cells = own.shape
    load_field(own, north, south, edges, turn, place_mid, place_north, place_south, flags, mid, rim)
    mask = mask_in[0:1, :]
    upstream = (total[...].astype(F32) * mask).astype(BF16)
    back[...] = dot(rw[...], upstream, 1, 0)
    convolve(mid, rim, weights, weights, spread, columns)
    field = spread[:channels, :]
    center = field - jnp.mean(field, axis=0, keepdims=True)
    rescale = lax.rsqrt(jnp.mean(center * center, axis=0, keepdims=True) + EPSILON)
    normal = center * rescale
    spread[:channels, :] = normal
    half = normal.astype(BF16)
    pre[...] = dot(ew[...], half, 0, 0)
    activate(pre, back, act, bp)
    back_normal = dot(ew[...], bp[...], 1, 0)
    normal = spread[:channels, :]
    mean_back = jnp.mean(back_normal, axis=0, keepdims=True)
    mean_cross = jnp.mean(back_normal * normal, axis=0, keepdims=True)
    back_spread = (rescale * (back_normal - mean_back - normal * mean_cross)).astype(BF16)
    back_out[...] = back_spread
    left_out[...] = dot(pick_left[...], back_spread, 1, 1).astype(BF16)
    right_out[...] = dot(pick_right[...], back_spread, 1, 1).astype(BF16)
    units = bp.shape[0]
    half_lanes = pack.shape[1] // 2
    pack[:units, :channels] = (dot(bp[...], normal.astype(BF16), 1, 1) * factor).astype(BF16)
    pack[:units, half_lanes : half_lanes + channels] = (dot(act[...], upstream, 1, 1) * factor).astype(BF16)
    update = dot(rw[...], act[...], 0, 0)
    one_out[...] = (one[...].astype(F32) - update * mask).astype(BF16)
    spread[:channels, :] = back_spread.astype(F32)
    correlate(mid, rim, spread, gk_wide, columns)
    spare = pack.shape[0] - units
    pick = lax.broadcasted_iota(jnp.int32, (spare, columns), 0) == lax.broadcasted_iota(jnp.int32, (spare, columns), 1)
    taps = (gk_wide[:channels, :] * factor).astype(BF16)
    pack[units:, :channels] = dot(jnp.where(pick, 1.0, 0.0).astype(BF16), taps, 1, 1).astype(BF16)


def back_kernel(
    columns, flags, own, north, south, edges, turn, place_mid, place_north, place_south,
    cot_two, weights, north_weights, out, mid, rim, through,
):
    channels, cells = own.shape
    load_field(own, north, south, edges, turn, place_mid, place_north, place_south, flags, mid, rim)
    convolve(mid, rim, weights, north_weights, through, columns)
    out[...] = (cot_two[...].astype(F32) + through[:channels, :]).astype(BF16)


def placements(rows, columns):
    cells = rows * columns
    pick_left = np.zeros((EDGE_ROWS, cells), np.float32)
    pick_right = np.zeros((EDGE_ROWS, cells), np.float32)
    place = np.zeros((2, EDGE_ROWS, cells), np.float32)
    folded = np.zeros((2, EDGE_ROWS, cells), np.float32)
    for r in range(rows):
        for c in range(REACH):
            e = r * REACH + c
            pick_left[e, r * columns + c] = 1
            pick_right[e, r * columns + columns - REACH + c] = 1
            place[0, e, r * columns + columns - REACH + c] = 1
            place[1, e, r * columns + c] = 1
            turned = rows - 1 - r
            folded[0, e, turned * columns + columns - 1 - c] = 1
            folded[1, e, turned * columns + REACH - 1 - c] = 1
    return pick_left, pick_right, place, folded


def body(
    output_one, output_two, cotan_one, cotan_two, wet_list, depth_kernel,
    expand_weight, reduce_weight, level_expand, level_reduce,
):
    channels, rows, columns = output_one.shape
    cells = rows * columns
    groups, levels, width = level_expand.shape
    hidden = expand_weight.shape[1]
    nx, ny = lax.axis_size("gx"), lax.axis_size("gy")
    factor = 1.0 / math.sqrt(cells * nx * ny)
    wide = -(-channels // 8) * 8
    slot = -(-width // 16) * 16
    i, j = lax.axis_index("gx"), lax.axis_index("gy")
    top = j == ny - 1
    flags = jnp.stack([(j > 0).astype(jnp.int32), top.astype(jnp.int32)])

    pick_left, pick_right, place, folded = [jnp.asarray(m, BF16) for m in placements(rows, columns)]
    place_north = jnp.where(top, folded, place)
    row_id = lax.broadcasted_iota(jnp.int32, (cells, cells), 0)
    col_id = lax.broadcasted_iota(jnp.int32, (cells, cells), 1)
    turn = jnp.where(jnp.where(top, cells - 1 - row_id, row_id) == col_id, 1.0, 0.0).astype(BF16)

    flat = lambda x: x.reshape(channels, cells)
    tile = jax.ShapeDtypeStruct((channels, cells), BF16)
    edge = jax.ShapeDtypeStruct((EDGE_ROWS, channels), BF16)
    vmem = pl.BlockSpec(memory_space=pltpu.VMEM)
    smem = pl.BlockSpec(memory_space=pltpu.SMEM)
    params = pltpu.CompilerParams(vmem_limit_bytes=56 * 1024 * 1024)

    one, two, cot_one, cot_two = flat(output_one), flat(output_two), flat(cotan_one), flat(cotan_two)
    two_in, total, left, right, mask, gle, glr = pl.pallas_call(
        functools.partial(level_kernel, factor, slot),
        out_shape=(
            tile, tile, edge, edge,
            jax.ShapeDtypeStruct((8, cells), F32),
            jax.ShapeDtypeStruct(level_expand.shape, F32),
            jax.ShapeDtypeStruct(level_reduce.shape, F32),
        ),
        in_specs=[vmem] * 9,
        out_specs=(vmem,) * 7,
        scratch_shapes=[pltpu.VMEM((channels, cells), F32)] * 4
        + [pltpu.VMEM((groups * slot, cells), F32)] * 2
        + [pltpu.VMEM((groups * slot, cells), BF16)] * 2,
        compiler_params=params,
        name="level",
    )(one, two, cot_one, cot_two, wet_list.reshape(-1, 1), level_expand, level_reduce, pick_left, pick_right)
    gle, glr = lax.psum((gle, glr), ("gx", "gy"))

    halo = pl.pallas_call(
        functools.partial(halo_kernel, nx, ny),
        out_shape=(tile, tile, jax.ShapeDtypeStruct((6, EDGE_ROWS, channels), BF16)),
        in_specs=[vmem] * 3,
        out_specs=(vmem,) * 3,
        scratch_shapes=[pltpu.SemaphoreType.DMA((11,)), pltpu.SemaphoreType.DMA((8,))],
        compiler_params=pltpu.CompilerParams(collective_id=0, has_side_effects=True),
        name="halo",
    )
    north, south, edges = halo(two_in, left, right)

    taps = depth_kernel.astype(F32).reshape(channels, TAPS * TAPS)
    pad = lambda w: jnp.pad(w, ((0, wide - channels), (0, 128 - TAPS * TAPS)))
    field_scratch = [pltpu.VMEM((3, wide, cells), F32)] * 2 + [pltpu.VMEM((wide, cells), F32)]
    chunks = nx * ny
    spare_rows = TAPS * TAPS
    chunk_rows = -(-(hidden + spare_rows) // (8 * chunks)) * 8
    half_lanes = -(-channels // 384) * 384
    lanes = 2 * half_lanes
    one_in, back, back_left, back_right, pack = pl.pallas_call(
        functools.partial(mixer_kernel, factor, columns),
        out_shape=(
            tile, tile, edge, edge,
            jax.ShapeDtypeStruct((chunks * chunk_rows, lanes), BF16),
        ),
        in_specs=[smem] + [vmem] * 16,
        out_specs=(vmem,) * 5,
        scratch_shapes=field_scratch
        + [pltpu.VMEM((hidden, cells), F32)] * 2
        + [pltpu.VMEM((hidden, cells), BF16)] * 2
        + [pltpu.VMEM((wide, 128), F32)],
        compiler_params=params,
        name="mixer",
    )(
        flags, two_in, north, south, edges, turn, place, place_north, place, one, total, mask,
        pad(taps), expand_weight, reduce_weight, pick_left, pick_right,
    )
    dims = [(1, k) for k in range(ny.bit_length() - 1)] + [(0, k) for k in range(nx.bit_length() - 1)]
    pack = pack.reshape(chunks, chunk_rows, lanes)
    summed = pl.pallas_call(
        functools.partial(sum_kernel, dims),
        out_shape=jax.ShapeDtypeStruct(pack.shape, BF16),
        in_specs=[vmem],
        out_specs=vmem,
        scratch_shapes=[
            pltpu.VMEM(pack.shape, BF16),
            pltpu.VMEM(pack.shape, BF16),
            pltpu.SemaphoreType.DMA((3, 2 * len(dims))),
            pltpu.SemaphoreType.DMA((3, 2 * len(dims))),
        ],
        compiler_params=pltpu.CompilerParams(
            collective_id=1, has_side_effects=True, vmem_limit_bytes=56 * 1024 * 1024
        ),
        name="sum",
    )(pack).reshape(chunks * chunk_rows, lanes)
    ge = summed[:hidden, :channels].T
    gr = summed[:hidden, half_lanes : half_lanes + channels]
    gk = summed[hidden : hidden + spare_rows, :channels].T

    north, south, edges = halo(back, back_left, back_right)
    flipped = taps[:, ::-1]
    grad_two = pl.pallas_call(
        functools.partial(back_kernel, columns),
        out_shape=tile,
        in_specs=[smem] + [vmem] * 11,
        out_specs=vmem,
        scratch_shapes=field_scratch,
        compiler_params=params,
        name="back",
    )(
        flags, back, north, south, edges, turn, place, place_north, place, cot_two,
        pad(flipped), pad(jnp.where(top, taps, flipped)),
    )
    grid = lambda x: x.reshape(channels, rows, columns)
    gk = gk[:, : TAPS * TAPS].astype(F32).reshape(channels, TAPS, TAPS)
    return (
        grid(one_in), grid(two_in), grid(total), grid(grad_two),
        gk, ge.astype(F32), gr.astype(F32), gle, glr,
    )


def solution(mesh):
    field = P(None, "gy", "gx")
    return jax.shard_map(
        body,
        mesh=mesh,
        in_specs=(field,) * 4 + (P("gy", "gx", None, None),) + (P(),) * 5,
        out_specs=(field,) * 4 + (P(),) * 5,
        check_vma=False,
    )
```
